32 devices in a mesh: row: 8 (over y, x, core), col: 4 (over z).
Axes of the slice: x: 2, y: 2, z: 4, core: 2. Of those that a mesh axis runs over, the one named last changes fastest.
Arguments:
- inputs: bfloat16 [32768, 261], P('row'), may hold values from -6 to 6
- latent: bfloat16 [512, 1024], P('row', 'col'), may hold values from -6 to 6
- gain_latent: float32 [1024], P('col'), may hold values from 0.25 to 1.75
- gain_inputs: float32 [261], replicated, may hold values from 0.25 to 1.75
- cross_query: bfloat16 [1024, 1024], P('col', 'row'), may hold values from -0.1875 to 0.1875
- cross_keys: bfloat16 [261, 1024], P(None, 'col'), may hold values from -0.375 to 0.375
- cross_values: bfloat16 [261, 1024], P(None, 'col'), may hold values from -0.375 to 0.375
- cross_output: bfloat16 [1024, 1024], P('col', 'row'), may hold values from -3 to 3
- cross_gain: float32 [1024], P('col'), may hold values from 0.25 to 1.75
- cross_up: bfloat16 [1024, 1024], P('row', 'col'), may hold values from -0.1875 to 0.1875
- cross_down: bfloat16 [1024, 1024], P('col', 'row'), may hold values from -0.1875 to 0.1875
- self_gain: float32 [1024], P('col'), may hold values from 0.25 to 1.75
- self_query: bfloat16 [1024, 1024], P('row', 'col'), may hold values from -0.1875 to 0.1875
- self_keys: bfloat16 [1024, 1024], P('row', 'col'), may hold values from -0.1875 to 0.1875
- self_values: bfloat16 [1024, 1024], P('row', 'col'), may hold values from -0.1875 to 0.1875
- self_output: bfloat16 [1024, 1024], P('col', 'row'), may hold values from -2 to 2
- self_mlp_gain: float32 [1024], P('col'), may hold values from 0.25 to 1.75
- self_mlp_up: bfloat16 [1024, 1024], P('row', 'col'), may hold values from -0.1875 to 0.1875
- self_mlp_down: bfloat16 [1024, 1024], P('col', 'row'), may hold values from -0.1875 to 0.1875
- cotangent: bfloat16 [16384, 1024], P('row', 'col'), may hold values from -6 to 6
Outputs:
- result: bfloat16 [16384, 1024], P('row', 'col')
- grad_inputs: float32 [32768, 261], P(('row', 'col'))
- grad_latent: float32 [512, 1024], P('row', 'col')
- grad_gain_latent: float32 [1024], P('col')
- grad_gain_inputs: float32 [261], replicated
- grad_cross_query: float32 [1024, 1024], P('col', 'row')
- grad_cross_keys: float32 [261, 1024], P(None, 'col')
- grad_cross_values: float32 [261, 1024], P(None, 'col')
- grad_cross_output: float32 [1024, 1024], P('col', 'row')
- grad_cross_gain: float32 [1024], P('col')
- grad_cross_up: float32 [1024, 1024], P('row', 'col')
- grad_cross_down: float32 [1024, 1024], P('col', 'row')
- grad_self_gain: float32 [1024], P('col')
- grad_self_query: float32 [1024, 1024], P('row', 'col')
- grad_self_keys: float32 [1024, 1024], P('row', 'col')
- grad_self_values: float32 [1024, 1024], P('row', 'col')
- grad_self_output: float32 [1024, 1024], P('col', 'row')
- grad_self_mlp_gain: float32 [1024], P('col')
- grad_self_mlp_up: float32 [1024, 1024], P('row', 'col')
- grad_self_mlp_down: float32 [1024, 1024], P('col', 'row')
The draws below stay inside these ranges and needn't reach their ends.
All inputs are finite; a program needn't handle non-finite values.
Results may differ from the reference program's by a relative error of at most 0.039.
Values may be sent and summed in bfloat16 or wider, within the bound.
No kernel may reach another device: no remote copies, remote signals or barrier semaphores. Data moves between devices by JAX's collectives and lax.ppermute only.
A program may use at most 192 MiB of HBM per device.

```python
import jax
import jax.numpy as jnp
from jax import lax

D = 1024
N = 512
C = 261
HEADS = 8
HEAD_DIM = 128
M = 1024
IMAGES = 32


def shard_levels(own_key, dims, split, least, high):
    def one(dim, shards_of):
        heights = jax.random.uniform(jax.random.fold_in(jax.random.fold_in(own_key, 6), dim), (shards_of,), jnp.float32, least / len(split), high / len(split))
        return jnp.repeat(jnp.exp(heights), dims[dim] // shards_of).reshape((-1,) + (1,) * (len(dims) - dim - 1))

    level = one(*split[0])
    for cut in split[1:]:
        level = level * one(*cut)
    return level


def noise(stream_key, dims, scale, limit, split=(), dtype=jnp.bfloat16):
    factor_of = shard_levels(stream_key, dims, split, -0.22, 0.18) if split else 1.0
    entries = jax.random.normal(stream_key, dims, jnp.float32) * scale * factor_of
    return jnp.minimum(jnp.maximum(entries, -limit), limit).astype(dtype)


def setup_inputs(seed: int = 0) -> dict:
    key_of = jax.random.split(jax.random.key(seed), 21)
    inputs = noise(key_of[0], (IMAGES * M, C), 1.0, 6.0, ((0, 8),))
    latent = noise(key_of[1], (N, D), 1.0, 6.0, ((0, 8), (1, 4)))
    gain_latent = jnp.clip(1.0 + 0.15 * jax.random.normal(key_of[2], (D,), jnp.float32), 0.25, 1.75)
    gain_inputs = jnp.clip(1.0 + 0.15 * jax.random.normal(key_of[3], (C,), jnp.float32), 0.25, 1.75)
    cross_query = noise(key_of[4], (D, D), D ** -0.5, 0.1875, ((0, 4), (1, 8)))
    cross_keys = noise(key_of[5], (C, D), C ** -0.5, 0.375, ((1, 4),))
    cross_values = noise(key_of[6], (C, D), C ** -0.5, 0.375, ((1, 4),))
    cross_output = noise(key_of[7], (D, D), (max(D // 256, 1)) ** -0.5, 3.0, ((0, 4), (1, 8)))
    cross_gain = jnp.clip(1.0 + 0.15 * jax.random.normal(key_of[8], (D,), jnp.float32), 0.25, 1.75)
    cross_up = noise(key_of[9], (D, D), D ** -0.5, 0.1875, ((0, 8), (1, 4)))
    cross_down = noise(key_of[10], (D, D), D ** -0.5, 0.1875, ((0, 4), (1, 8)))
    self_gain = jnp.clip(1.0 + 0.15 * jax.random.normal(key_of[11], (D,), jnp.float32), 0.25, 1.75)
    self_query = noise(key_of[12], (D, D), D ** -0.5, 0.1875, ((0, 8), (1, 4)))
    self_keys = noise(key_of[13], (D, D), D ** -0.5, 0.1875, ((0, 8), (1, 4)))
    self_values = noise(key_of[14], (D, D), D ** -0.5, 0.1875, ((0, 8), (1, 4)))
    self_output = noise(key_of[15], (D, D), (max(D // 128, 1)) ** -0.5, 2.0, ((0, 4), (1, 8)))
    self_mlp_gain = jnp.clip(1.0 + 0.15 * jax.random.normal(key_of[16], (D,), jnp.float32), 0.25, 1.75)
    self_mlp_up = noise(key_of[17], (D, D), D ** -0.5, 0.1875, ((0, 8), (1, 4)))
    self_mlp_down = noise(key_of[18], (D, D), D ** -0.5, 0.1875, ((0, 4), (1, 8)))
    cotangent = noise(key_of[19], (IMAGES * N, D), 1.0, 6.0, ((0, 8), (1, 4)))
    return {"inputs": inputs, "latent": latent, "gain_latent": gain_latent, "gain_inputs": gain_inputs, "cross_query": cross_query, "cross_keys": cross_keys, "cross_values": cross_values, "cross_output": cross_output, "cross_gain": cross_gain, "cross_up": cross_up, "cross_down": cross_down, "self_gain": self_gain, "self_query": self_query, "self_keys": self_keys, "self_values": self_values, "self_output": self_output, "self_mlp_gain": self_mlp_gain, "self_mlp_up": self_mlp_up, "self_mlp_down": self_mlp_down, "cotangent": cotangent}


epsilon = 1e-05
highest = lax.Precision.HIGHEST

@jax.custom_vjp
def low(v):
    return lax.optimization_barrier(v.astype(jnp.bfloat16)).astype(jnp.float32)

@jax.custom_vjp
def low_back(v):
    return v

def low_keep(v):
    return (low(v), None)

def low_pass(kept, grad):
    return (grad,)

def back_keep(v):
    return (v, None)

def back_low(kept, grad):
    return (low(grad),)
low.defvjp(low_keep, low_pass)
low_back.defvjp(back_keep, back_low)

def matmul_high(left_side, right_side):
    return jnp.dot(left_side, right_side, precision=highest)

def norm_rows(values, gain):
    average = lax.optimization_barrier(jnp.mean(values, axis=-1, keepdims=True))
    centred = values - average
    spread = lax.optimization_barrier(jnp.mean(centred * centred, axis=-1, keepdims=True))
    return centred * lax.rsqrt(spread + epsilon) * gain

def softmax_rows(scores):
    peak_value = lax.optimization_barrier(jnp.max(scores, axis=-1, keepdims=True))
    exponent = jnp.exp(scores - peak_value)
    return exponent / lax.optimization_barrier(jnp.sum(exponent, axis=-1, keepdims=True))

def gelu_value(values):
    return jax.nn.gelu(values, approximate=True)

def one_image(weights, lat_low, lat_value, pixels):
    gain_inputs, cross_query, cross_keys, cross_values, cross_output, cross_gain, cross_up, cross_down, self_gain, self_query, self_keys, self_values, self_output, self_mlp_gain, self_mlp_up, self_mlp_down = weights
    query_rows = low_back(low(matmul_high(lat_low, cross_query)))
    pix_low = low(norm_rows(pixels, gain_inputs))
    key_rows = low_back(low(matmul_high(pix_low, cross_keys)))
    values = low_back(low(matmul_high(pix_low, cross_values)))
    scores = low_back(matmul_high(query_rows, key_rows.T) * D ** (-0.5))
    soft_scores = low(softmax_rows(scores))
    attended = low_back(low(matmul_high(soft_scores, values)))
    state_one = lat_value + low_back(matmul_high(attended, cross_output))
    hidden = low_back(matmul_high(low(norm_rows(state_one, cross_gain)), cross_up))
    state_two = state_one + low_back(matmul_high(low(gelu_value(hidden)), cross_down))
    attn_low = low(norm_rows(state_two, self_gain))
    head_q = low_back(low(matmul_high(attn_low, self_query))).reshape(N, HEADS, HEAD_DIM)
    head_k = low_back(low(matmul_high(attn_low, self_keys))).reshape(N, HEADS, HEAD_DIM)
    head_v = low_back(low(matmul_high(attn_low, self_values))).reshape(N, HEADS, HEAD_DIM)
    self_scores = low_back(jnp.einsum('qhd,khd->hqk', head_q, head_k, precision=highest) * HEAD_DIM ** (-0.5))
    self_soft = low(softmax_rows(self_scores))
    self_att = low_back(low(jnp.einsum('hqk,khd->qhd', self_soft, head_v, precision=highest).reshape(N, D)))
    state_three = state_two + low_back(matmul_high(self_att, self_output))
    hidden_two = low_back(matmul_high(low(norm_rows(state_three, self_mlp_gain)), self_mlp_up))
    return state_three + low_back(matmul_high(low(gelu_value(hidden_two)), self_mlp_down))

def forward(lat_value, gain_latent, weights, pixels_all):
    lat_low = low(norm_rows(lat_value, gain_latent))

    def per_image(pixels):
        return one_image(weights, lat_low, lat_value, pixels)
    return lax.map(jax.checkpoint(per_image), pixels_all)

def reference(inputs, latent, gain_latent, gain_inputs, cross_query, cross_keys, cross_values, cross_output, cross_gain, cross_up, cross_down, self_gain, self_query, self_keys, self_values, self_output, self_mlp_gain, self_mlp_up, self_mlp_down, cotangent):
    weights = tuple((item.astype(jnp.float32) for item in (gain_inputs, cross_query, cross_keys, cross_values, cross_output, cross_gain, cross_up, cross_down, self_gain, self_query, self_keys, self_values, self_output, self_mlp_gain, self_mlp_up, self_mlp_down)))
    pixels_all = inputs.astype(jnp.float32).reshape(IMAGES, M, C)
    lat_value = latent.astype(jnp.float32)
    outputs, pull_back = jax.vjp(forward, lat_value, gain_latent.astype(jnp.float32), weights, pixels_all)
    grad_lat, grad_gain_lat, grad_weights, grad_pixels = pull_back(cotangent.astype(jnp.float32).reshape(IMAGES, N, D))
    g_inputs_gain, g_cq, g_ck, g_cv, g_co, g_cg, g_cu, g_cd, g_sg, g_sq, g_sk, g_sv, g_so, g_smg, g_smu, g_smd = grad_weights
    return (outputs.reshape(IMAGES * N, D).astype(jnp.bfloat16), grad_pixels.reshape(IMAGES * M, C), grad_lat, grad_gain_lat, g_inputs_gain, g_cq, g_ck, g_cv, g_co, g_cg, g_cu, g_cd, g_sg, g_sq, g_sk, g_sv, g_so, g_smg, g_smu, g_smd)
```

```python
import jax
import jax.numpy as jnp
from jax import lax
from jax.sharding import PartitionSpec as P

HEADS = 8
M = 1024
EPSILON = 1e-05
BF = jnp.bfloat16
F32 = jnp.float32
BOTH = ("row", "col")


def nn(left, right):
    return lax.dot_general(left, right, (((1,), (0,)), ((), ())), preferred_element_type=F32)


def nt(left, right):
    return lax.dot_general(left, right, (((1,), (1,)), ((), ())), preferred_element_type=F32)


def tn(left, right):
    return lax.dot_general(left, right, (((0,), (0,)), ((), ())), preferred_element_type=F32)


def norm(values, gain):
    average = jnp.mean(values, axis=-1, keepdims=True)
    centred = values - average
    scale = lax.rsqrt(jnp.mean(centred * centred, axis=-1, keepdims=True) + EPSILON)
    hat = centred * scale
    return (hat * gain).astype(BF), hat, scale


def norm_back(upstream, gain, hat, scale):
    scaled = upstream * gain
    first = jnp.mean(scaled, axis=-1, keepdims=True)
    second = jnp.mean(scaled * hat, axis=-1, keepdims=True)
    return scale * (scaled - first - hat * second), jnp.sum(upstream * hat, axis=0)


def gelu(values):
    return jax.nn.gelu(values, approximate=True)


def gelu_back(values, upstream):
    return jax.vjp(gelu, values)[1](upstream)[0].astype(BF)


def softmax(scores):
    exponent = jnp.exp(scores - jnp.max(scores, axis=-1, keepdims=True))
    return exponent / jnp.sum(exponent, axis=-1, keepdims=True)


def softmax_back(soft, upstream):
    return (soft * (upstream - jnp.sum(upstream * soft, axis=-1, keepdims=True))).astype(BF)


def local(
    inputs,
    latent,
    gain_latent,
    gain_inputs,
    cross_query,
    cross_keys,
    cross_values,
    cross_output,
    cross_gain,
    cross_up,
    cross_down,
    self_gain,
    self_query,
    self_keys,
    self_values,
    self_output,
    self_mlp_gain,
    self_mlp_up,
    self_mlp_down,
    cotangent,
):
    cols = lax.axis_size("col")
    rows = lax.axis_size("row")
    place = lax.axis_index("col")
    wide = latent.shape[1] * cols
    block = latent.shape[1]
    lat_count = latent.shape[0] * rows
    head_size = wide // HEADS
    in_width = inputs.shape[1]
    images = inputs.shape[0] // M
    share = max(1, cols // images)
    assert images * share == cols
    here = lat_count // share
    groups = [[image * share + part for part in range(share)] for image in range(images)]
    cross_scale = wide ** (-0.5)
    self_scale = head_size ** (-0.5)

    by_row = (cross_up, self_query, self_keys, self_values, self_mlp_up)
    by_col = (cross_query, cross_output, cross_down, self_output, self_mlp_down)
    stack = jnp.stack([item.T for item in by_col] + list(by_row))
    count = stack.shape[0]
    deep = stack.shape[1]
    whole = lax.all_gather(stack, BOTH, axis=0, tiled=False)
    whole = whole.reshape(rows, cols, count, deep, block)
    whole = whole.transpose(2, 0, 3, 1, 4).reshape(count, wide, wide)
    t_query, t_output, t_down, t_self_output, t_self_down, up, s_query, s_keys, s_values, s_up = [
        whole[index] for index in range(count)
    ]
    lat_all = lax.all_gather(latent, BOTH, axis=0, tiled=False)
    lat_all = lat_all.reshape(rows, cols, -1, block).transpose(0, 2, 1, 3).reshape(lat_count, wide)
    pair = lax.all_gather(jnp.concatenate([cross_keys, cross_values]), "col", axis=1, tiled=True)
    c_keys, c_values = pair[:in_width], pair[in_width:]
    gains = lax.all_gather(
        jnp.stack([gain_latent, cross_gain, self_gain, self_mlp_gain]), "col", axis=1, tiled=True
    )
    g_lat, g_cross, g_self, g_mlp = [gains[index] for index in range(4)]
    grad_out_low = lax.all_to_all(cotangent, "col", split_axis=0, concat_axis=1, tiled=True)

    start = (place % share) * here
    lat = lax.dynamic_slice_in_dim(lat_all, start, here, axis=0).astype(F32)
    pixels = lax.dynamic_slice_in_dim(inputs, (place // share) * M, M, axis=0).astype(F32)

    lat_low, lat_hat, lat_scale = norm(lat, g_lat)
    queries = nt(lat_low, t_query).astype(BF)
    pix_low, pix_hat, pix_scale = norm(pixels, gain_inputs)
    key_rows = nn(pix_low, c_keys).astype(BF)
    values = nn(pix_low, c_values).astype(BF)
    soft = softmax(nt(queries, key_rows) * cross_scale)
    soft_low = soft.astype(BF)
    attended = nn(soft_low, values).astype(BF)
    state_one = lat + nt(attended, t_output)
    mlp_low, mlp_hat, mlp_scale = norm(state_one, g_cross)
    hidden = nn(mlp_low, up)
    active = gelu(hidden).astype(BF)
    state_two = state_one + nt(active, t_down)
    attn_low, attn_hat, attn_scale = norm(state_two, g_self)
    head_q = nn(attn_low, s_query).astype(BF)
    head_k = nn(attn_low, s_keys).astype(BF)
    head_v = nn(attn_low, s_values).astype(BF)
    if share > 1:
        head_k, head_v = [
            lax.all_gather(item, "col", axis_index_groups=groups, axis=0, tiled=True)
            for item in (head_k, head_v)
        ]

    def split(item):
        return item.reshape(item.shape[0], HEADS, head_size)

    def join(item):
        return item.astype(BF).reshape(item.shape[0], wide)

    def contract(form, left, right):
        return jnp.einsum(form, left, right, preferred_element_type=F32)

    hq, hk, hv = split(head_q), split(head_k), split(head_v)
    self_soft = softmax(contract("qhd,khd->hqk", hq, hk) * self_scale)
    self_soft_low = self_soft.astype(BF)
    self_att = join(contract("hqk,khd->qhd", self_soft_low, hv))
    state_three = state_two + nt(self_att, t_self_output)
    last_low, last_hat, last_scale = norm(state_three, g_mlp)
    hidden_two = nn(last_low, s_up)
    active_two = gelu(hidden_two).astype(BF)
    result = (state_three + nt(active_two, t_self_down)).astype(BF)
    result = lax.all_to_all(result, "col", split_axis=1, concat_axis=0, tiled=True)

    grad_self_down = tn(grad_out_low, active_two)
    dh2 = gelu_back(hidden_two, nn(grad_out_low, t_self_down))
    grad_self_up = tn(last_low, dh2)
    back, gain_mlp = norm_back(nt(dh2, s_up), g_mlp, last_hat, last_scale)
    g3 = grad_out_low.astype(F32) + back
    g3_low = g3.astype(BF)
    grad_self_output = tn(g3_low, self_att)
    d_att = split(nn(g3_low, t_self_output).astype(BF))
    d_self = softmax_back(self_soft, contract("qhd,khd->hqk", d_att, hv))
    dq = join(contract("hqk,khd->qhd", d_self, hk) * self_scale)
    dk = contract("hqk,qhd->khd", d_self, hq) * self_scale
    dvv = contract("hqk,qhd->khd", self_soft_low, d_att)
    dk, dvv = join(dk), join(dvv)
    if share > 1:
        dk, dvv = [
            lax.psum_scatter(
                item, "col", axis_index_groups=groups, scatter_dimension=0, tiled=True
            )
            for item in (dk, dvv)
        ]
    grad_query, grad_keys, grad_values = tn(attn_low, dq), tn(attn_low, dk), tn(attn_low, dvv)
    dy = nt(dq, s_query) + nt(dk, s_keys) + nt(dvv, s_values)
    back, gain_self = norm_back(dy, g_self, attn_hat, attn_scale)
    g2 = g3 + back
    g2_low = g2.astype(BF)
    grad_down = tn(g2_low, active)
    dh1 = gelu_back(hidden, nn(g2_low, t_down))
    grad_up = tn(mlp_low, dh1)
    back, gain_cross = norm_back(nt(dh1, up), g_cross, mlp_hat, mlp_scale)
    g1 = g2 + back
    g1_low = g1.astype(BF)
    grad_output = tn(g1_low, attended)
    d_attended = nn(g1_low, t_output).astype(BF)
    d_scores = softmax_back(soft, nt(d_attended, values))
    d_queries = (nn(d_scores, key_rows) * cross_scale).astype(BF)
    d_keys = (tn(d_scores, queries) * cross_scale).astype(BF)
    d_values = tn(soft_low, d_attended).astype(BF)
    grad_cross_query = tn(d_queries, lat_low)
    grad_pair = jnp.concatenate([tn(pix_low, d_keys), tn(pix_low, d_values)])
    d_pix = nt(d_keys, c_keys) + nt(d_values, c_values)
    grad_inputs, gain_pix = norm_back(d_pix, gain_inputs, pix_hat, pix_scale)
    if share > 1:
        grad_inputs = lax.psum_scatter(
            grad_inputs, "col", axis_index_groups=groups, scatter_dimension=0, tiled=True
        )
    back, gain_lat = norm_back(nn(d_queries, t_query), g_lat, lat_hat, lat_scale)
    grad_lat = g1 + back
    if share > 1:
        grad_lat = lax.dynamic_update_slice_in_dim(
            jnp.zeros((lat_count, wide), F32), grad_lat, start, axis=0
        )

    def reduce(item):
        item = lax.psum_scatter(item, "row", scatter_dimension=0, tiled=False)
        return lax.psum_scatter(item, "col", scatter_dimension=0, tiled=False).astype(F32)

    grads = jnp.stack(
        [
            item.astype(BF)
            for item in (
                grad_cross_query,
                grad_output,
                grad_down,
                grad_self_output,
                grad_self_down,
                grad_up,
                grad_query,
                grad_keys,
                grad_values,
                grad_self_up,
            )
        ]
    )
    grads = grads.reshape(count, rows, deep, cols, block).transpose(1, 3, 0, 2, 4)
    grads = reduce(grads)
    grad_lat = reduce(
        grad_lat.astype(BF).reshape(rows, -1, cols, block).transpose(0, 2, 1, 3)
    )
    grad_pair = lax.psum_scatter(
        grad_pair.astype(BF).reshape(-1, cols, block).transpose(1, 0, 2),
        "col",
        scatter_dimension=0,
        tiled=False,
    )
    grad_pair = lax.psum(grad_pair, "row").astype(F32)
    gain_all, gain_pix = lax.psum(
        (jnp.stack([gain_lat, gain_cross, gain_self, gain_mlp]), gain_pix), BOTH
    )
    gain_all = lax.dynamic_slice_in_dim(gain_all, place * block, block, axis=1)
    return (
        result,
        grad_inputs,
        grad_lat,
        gain_all[0],
        gain_pix,
        grads[0].T,
        grad_pair[:in_width],
        grad_pair[in_width:],
        grads[1].T,
        gain_all[1],
        grads[5],
        grads[2].T,
        gain_all[2],
        grads[6],
        grads[7],
        grads[8],
        grads[3].T,
        gain_all[3],
        grads[9],
        grads[4].T,
    )


def solution(mesh):
    rc, cr, c, cc = P("row", "col"), P("col", "row"), P("col"), P(None, "col")
    return jax.shard_map(
        local,
        mesh=mesh,
        in_specs=(
            P("row", None), rc, c, P(), cr, cc, cc, cr, c, rc, cr, c, rc, rc, rc, cr, c, rc, cr, rc,
        ),
        out_specs=(
            rc, P(BOTH, None), rc, c, P(), cr, cc, cc, cr, c, rc, cr, c, rc, rc, rc, cr, c, rc, cr,
        ),
        check_vma=False,
    )
```
